32 devices in a mesh: parts: 2 (over y), patch: 4 (over z), sub: 2 (over x), lvl: 2 (over core).
Axes of the slice: x: 2, y: 2, z: 4, core: 2. Of those that a mesh axis runs over, the one named last changes fastest.
Arguments:
- node_states: float32 [8192, 512], P(('parts', 'patch', 'lvl')), parts along dimension 0, may hold values from -6 to 6
- coarse_states: float32 [1024, 512], P(('parts', 'patch', 'lvl')), parts along dimension 0, may hold values from -6 to 6
- children: int32 [512, 7], P(('patch', 'lvl')), may hold values from 0 to 511
- down_sources: int32 [4096, 3], P(('patch', 'lvl')), may hold values from 0 to 63
- bottom_links: int32 [4096, 6], P(('patch', 'lvl')), may hold values from 0 to 767, as said below
- coarse_links: int32 [512, 6], P(('patch', 'lvl')), may hold values from 0 to 511
- upward_sender: float32 [512, 512], P(None, 'sub'), may hold values from -0.25 to 0.25
- upward_receiver: float32 [512, 512], P(None, 'sub'), may hold values from -0.25 to 0.25
- upward_bias: float32 [512], P('sub'), may hold values from -4 to 4
- upward_output: float32 [512, 512], P('sub'), may hold values from -0.25 to 0.25
- upward_gain: float32 [512], replicated, may hold values from 0.1 to 1.9
- coarse_sender: float32 [512, 512], P(None, 'sub'), may hold values from -0.25 to 0.25
- coarse_receiver: float32 [512, 512], P(None, 'sub'), may hold values from -0.25 to 0.25
- coarse_bias: float32 [512], P('sub'), may hold values from -4 to 4
- coarse_output: float32 [512, 512], P('sub'), may hold values from -0.25 to 0.25
- coarse_gain: float32 [512], replicated, may hold values from 0.1 to 1.9
- downward_sender: float32 [512, 512], P(None, 'sub'), may hold values from -0.25 to 0.25
- downward_receiver: float32 [512, 512], P(None, 'sub'), may hold values from -0.25 to 0.25
- downward_bias: float32 [512], P('sub'), may hold values from -4 to 4
- downward_output: float32 [512, 512], P('sub'), may hold values from -0.25 to 0.25
- downward_gain: float32 [512], replicated, may hold values from 0.1 to 1.9
- bottom_sender: float32 [512, 512], P(None, 'sub'), may hold values from -0.25 to 0.25
- bottom_receiver: float32 [512, 512], P(None, 'sub'), may hold values from -0.25 to 0.25
- bottom_bias: float32 [512], P('sub'), may hold values from -4 to 4
- bottom_output: float32 [512, 512], P('sub'), may hold values from -0.25 to 0.25
- bottom_gain: float32 [512], replicated, may hold values from 0.1 to 1.9
Outputs:
- new_nodes: float32 [8192, 512], P(('parts', 'patch', 'lvl')), parts along dimension 0
- new_coarse: float32 [1024, 512], P(('parts', 'patch', 'lvl')), parts along dimension 0
The draws below stay inside these ranges and needn't reach their ends.
There are 2 independent parts, one for each index of `parts`. The reference program is written for one: setup_inputs(seed, part) draws one part's arguments, and reference() takes and returns one part's arrays. A program takes and returns all parts, laid end to end along the dimension named above; an argument that names none is the same for every part. Nothing has to cross between parts.
Inputs may be any that keep to these rules, and one draw needn't show every extreme that they name: bottom_links[n, k] - 128 differs from n's row within its block by at most 128.
All inputs are finite; a program needn't handle non-finite values.
Results may differ from the reference program's by a relative error of at most 0.00011.
Values sent between devices are 32-bit elements; how exact they have to be, the bound alone decides.
A program may use at most 64 MiB of HBM per device.

```python
import jax
import jax.numpy as jnp
from jax import lax

LAT = 512
HID = 512
ROWS_DEV = 512
DEG = 6
CDEG = 6
UP = 7
DOWN = 3
HALO = 128
CDEV = 64
NB = 4096
NC = 512


def draw_children(key, part):
    factor = ROWS_DEV // CDEV
    position = jnp.arange(NC, dtype=jnp.int32) % CDEV
    offsets = jax.random.randint(key, (NC, UP), -4, 12, dtype=jnp.int32)
    result = jnp.clip(factor * position[:, None] + offsets, 0, ROWS_DEV - 1)
    result = result.at[0, 0].set(0).at[NC - 1, 0].set(ROWS_DEV - 1)
    return result.astype(jnp.int32)


def draw_down_sources(key, part):
    factor = ROWS_DEV // CDEV
    position = jnp.arange(NB, dtype=jnp.int32) % ROWS_DEV
    offsets = jax.random.randint(key, (NB, DOWN), -1, 2, dtype=jnp.int32)
    result = jnp.clip((position // factor)[:, None] + offsets, 0, CDEV - 1)
    result = result.at[0, 0].set(0).at[NB - 1, 0].set(CDEV - 1)
    return result.astype(jnp.int32)


def draw_bottom_links(key, part):
    position = jnp.arange(NB, dtype=jnp.int32) % ROWS_DEV
    offsets = jax.random.randint(key, (NB, DEG), -HALO, HALO + 1, dtype=jnp.int32)
    offsets = jnp.where(offsets == 0, 1, offsets)
    result = HALO + position[:, None] + offsets
    result = result.at[0, 0].set(0).at[NB - 1, 0].set(ROWS_DEV + 2 * HALO - 1)
    return result.astype(jnp.int32)


def draw_coarse_links(key, part):
    blocks = NC // CDEV
    first_key, second_key = jax.random.split(key)
    within = jax.random.randint(first_key, (NC, CDEG), 0, CDEV, dtype=jnp.int32)
    anywhere = jax.random.randint(second_key, (NC, CDEG), 0, blocks, dtype=jnp.int32)
    owning = (jnp.arange(NC, dtype=jnp.int32) // CDEV)[:, None]
    column = jnp.arange(CDEG, dtype=jnp.int32)[None, :]
    shifted = jnp.where(column == 0, owning, jnp.where(column == 1, owning + 1, jnp.where(column == 2, owning - 1 + blocks, owning + blocks // 2)))
    target = jnp.where(column < 4, shifted % blocks, anywhere)
    result = target * CDEV + within
    result = result.at[0, 0].set(0).at[NC - 1, 0].set(NC - 1)
    return result.astype(jnp.int32)


def block_levels(stream_key, extent, cuts, least, largest):
    loudness, own = 1.0, jax.random.fold_in(stream_key, 6)
    for dim, parts in cuts:
        heights = jnp.exp(jax.random.uniform(jax.random.fold_in(own, dim), (parts,), jnp.float32, least / len(cuts), largest / len(cuts)))
        loudness = loudness * jnp.repeat(heights, extent[dim] // parts).reshape([-1 if axis == dim else 1 for axis in range(len(extent))])
    return loudness


def normal_values(stream_key, extent, deviation, limit, shards=(), kind=jnp.bfloat16):
    factor_of = block_levels(stream_key, extent, shards, -0.22, 0.18) if shards else 1.0
    entries = jax.random.normal(stream_key, extent, jnp.float32) * deviation * factor_of
    return jnp.minimum(jnp.maximum(entries, -limit), limit).astype(kind)


def setup_inputs(seed: int = 0, part: int = 0) -> dict:
    streams_of = jax.random.split(jax.random.key(seed), 27)
    own_keys = jax.random.split(jax.random.fold_in(streams_of[26], part), 27)
    return {
        "node_states": normal_values(own_keys[0], (NB, LAT), 1.0, 6.0, ((0, 8),), jnp.float32),
        "coarse_states": normal_values(own_keys[1], (NC, LAT), 1.0, 6.0, ((0, 8),), jnp.float32),
        "children": draw_children(jax.random.fold_in(streams_of[26], 71), part),
        "down_sources": draw_down_sources(jax.random.fold_in(streams_of[26], 71), part),
        "bottom_links": draw_bottom_links(jax.random.fold_in(streams_of[26], 71), part),
        "coarse_links": draw_coarse_links(jax.random.fold_in(streams_of[26], 71), part),
        "upward_sender": normal_values(streams_of[6], (LAT, HID), LAT ** -0.5, 0.25, ((1, 2),), jnp.float32),
        "upward_receiver": normal_values(streams_of[7], (LAT, HID), LAT ** -0.5, 0.25, ((1, 2),), jnp.float32),
        "upward_bias": normal_values(streams_of[8], (HID,), 1.0, 4.0, ((0, 2),), jnp.float32),
        "upward_output": normal_values(streams_of[9], (HID, LAT), HID ** -0.5, 0.25, ((0, 2),), jnp.float32),
        "upward_gain": jnp.clip(1.0 + 0.18 * jax.random.normal(streams_of[10], (LAT,), jnp.float32), 0.1, 1.9),
        "coarse_sender": normal_values(streams_of[11], (LAT, HID), LAT ** -0.5, 0.25, ((1, 2),), jnp.float32),
        "coarse_receiver": normal_values(streams_of[12], (LAT, HID), LAT ** -0.5, 0.25, ((1, 2),), jnp.float32),
        "coarse_bias": normal_values(streams_of[13], (HID,), 1.0, 4.0, ((0, 2),), jnp.float32),
        "coarse_output": normal_values(streams_of[14], (HID, LAT), HID ** -0.5, 0.25, ((0, 2),), jnp.float32),
        "coarse_gain": jnp.clip(1.0 + 0.18 * jax.random.normal(streams_of[15], (LAT,), jnp.float32), 0.1, 1.9),
        "downward_sender": normal_values(streams_of[16], (LAT, HID), LAT ** -0.5, 0.25, ((1, 2),), jnp.float32),
        "downward_receiver": normal_values(streams_of[17], (LAT, HID), LAT ** -0.5, 0.25, ((1, 2),), jnp.float32),
        "downward_bias": normal_values(streams_of[18], (HID,), 1.0, 4.0, ((0, 2),), jnp.float32),
        "downward_output": normal_values(streams_of[19], (HID, LAT), HID ** -0.5, 0.25, ((0, 2),), jnp.float32),
        "downward_gain": jnp.clip(1.0 + 0.18 * jax.random.normal(streams_of[20], (LAT,), jnp.float32), 0.1, 1.9),
        "bottom_sender": normal_values(streams_of[21], (LAT, HID), LAT ** -0.5, 0.25, ((1, 2),), jnp.float32),
        "bottom_receiver": normal_values(streams_of[22], (LAT, HID), LAT ** -0.5, 0.25, ((1, 2),), jnp.float32),
        "bottom_bias": normal_values(streams_of[23], (HID,), 1.0, 4.0, ((0, 2),), jnp.float32),
        "bottom_output": normal_values(streams_of[24], (HID, LAT), HID ** -0.5, 0.25, ((0, 2),), jnp.float32),
        "bottom_gain": jnp.clip(1.0 + 0.18 * jax.random.normal(streams_of[25], (LAT,), jnp.float32), 0.1, 1.9),
    }


epsilon = 1e-05
highest = lax.Precision.HIGHEST

def project(states, weights):
    return jnp.dot(states, weights, precision=highest, preferred_element_type=jnp.float32)

def layer_norm(values):
    center = values - lax.optimization_barrier(jnp.mean(values, axis=-1, keepdims=True))
    spread = lax.optimization_barrier(jnp.mean(center * center, axis=-1, keepdims=True))
    return center * lax.rsqrt(spread + epsilon)

def interact(senders, receivers, link_index, sender_weights, receiver_weights, bias_vector, output_weights, gain_vector):
    sender_rows = project(senders, sender_weights)
    receiver_rows = project(receivers, receiver_weights) + bias_vector
    hidden = jnp.zeros_like(receiver_rows)
    for column in range(link_index.shape[1]):
        hidden = hidden + jax.nn.silu(sender_rows[link_index[:, column]] + receiver_rows)
    update = project(hidden, output_weights)
    return receivers + gain_vector * layer_norm(update)

def reference(node_states, coarse_states, children, down_sources, bottom_links, coarse_links, upward_sender, upward_receiver, upward_bias, upward_output, upward_gain, coarse_sender, coarse_receiver, coarse_bias, coarse_output, coarse_gain, downward_sender, downward_receiver, downward_bias, downward_output, downward_gain, bottom_sender, bottom_receiver, bottom_bias, bottom_output, bottom_gain):
    coarse_block = (jnp.arange(NC, dtype=jnp.int32) // CDEV)[:, None]
    child_index = (coarse_block * ROWS_DEV + children).astype(jnp.int32)
    node_block = (jnp.arange(NB, dtype=jnp.int32) // ROWS_DEV)[:, None]
    down_index = (node_block * CDEV + down_sources).astype(jnp.int32)
    mesh_index = ((node_block * ROWS_DEV + bottom_links - HALO) % NB).astype(jnp.int32)
    coarse_up = interact(node_states, coarse_states, child_index, upward_sender, upward_receiver, upward_bias, upward_output, upward_gain)
    new_coarse = interact(coarse_up, coarse_up, coarse_links, coarse_sender, coarse_receiver, coarse_bias, coarse_output, coarse_gain)
    nodes_down = interact(new_coarse, node_states, down_index, downward_sender, downward_receiver, downward_bias, downward_output, downward_gain)
    new_nodes = interact(nodes_down, nodes_down, mesh_index, bottom_sender, bottom_receiver, bottom_bias, bottom_output, bottom_gain)
    return (new_nodes, new_coarse)
```

```python
import functools

import jax
import jax.numpy as jnp
from jax import lax
from jax.experimental import pallas as pl
from jax.experimental.pallas import tpu as pltpu
from jax.sharding import PartitionSpec as P

epsilon = 1e-05
f32 = jnp.float32
bf16 = jnp.bfloat16
MESH = pl.DeviceIdType.MESH


def split(x):
    high = x.astype(bf16)
    return high, (x - high.astype(f32)).astype(bf16)


def mm(a, b):
    return jnp.dot(a, b, preferred_element_type=f32)


def dot3(x, w):
    return mm(x[0], w[0]) + (mm(x[0], w[1]) + mm(x[1], w[0]))


def layer_norm(values):
    center = values - jnp.mean(values, axis=-1, keepdims=True)
    spread = jnp.mean(center * center, axis=-1, keepdims=True)
    return center * lax.rsqrt(spread + epsilon)


def silu(v):
    h = 0.5 * v
    return h + h * jnp.tanh(h)


def joined(pair):
    return jnp.concatenate(pair, axis=1)


def pick(column, table, base):
    count, width = table.shape[0], table.shape[1] // 2
    lanes = lax.broadcasted_iota(jnp.int32, (column.shape[0], count), 1)
    hot = jnp.where(lanes == column - base, 1.0, 0.0).astype(bf16)
    rows = mm(hot, table)
    return rows[:, :width] + rows[:, width:]


def kernel(
    n_patch,
    n_sub,
    n_lvl,
    rim,
    tile,
    nodes_hbm,
    coarse_hbm,
    us_hbm, ur_hbm, uo_hbm,
    cs_hbm, cr_hbm, co_hbm,
    ds_hbm, dr_hbm, do_hbm,
    bs_hbm, br_hbm, bo_hbm,
    children, down_sources, bottom_links, coarse_links,
    ub, ug, cb, cg, db, dg, bb, bg,
    out_nodes,
    out_coarse,
    ns, cs, w_in, w_mid, wo_full, wo_pair, bw_pair,
    ns_pair, rd, rb, nd, ext, halo_out, halo_in,
    table, parts, hidden,
    load_sem, wo_send, wo_recv, fw_send, fw_recv,
    part_send, part_recv, tab_send, tab_recv, rel_send, rel_recv,
    hid_send, hid_recv, halo_send, halo_recv,
):
    patch = lax.axis_index("patch")
    sub = lax.axis_index("sub")
    lvl = lax.axis_index("lvl")
    rows = ns.shape[0]
    width = table.shape[2]
    tiles = rows // tile
    block = patch * n_lvl + lvl
    blocks = n_patch * n_lvl

    def at_sub(o):
        return {"sub": lax.rem(sub + o, n_sub)}

    def at_lvl(o):
        return {"lvl": lax.rem(lvl + o, n_lvl)}

    def at_patch(o):
        return {"patch": lax.rem(patch + o, n_patch)}

    def at_block(o):
        other = lax.rem(block + o + blocks, blocks)
        return {"patch": other // n_lvl, "lvl": lax.rem(other, n_lvl)}

    def from_sub(o):
        return lax.rem(sub - o + n_sub, n_sub)

    def from_patch(o):
        return lax.rem(patch - o + n_patch, n_patch)

    def from_lvl(o):
        return lax.rem(lvl - o + n_lvl, n_lvl)

    def remote(src, dst, send, recv, device):
        return pltpu.make_async_remote_copy(
            src_ref=src, dst_ref=dst, send_sem=send, recv_sem=recv,
            device_id=device, device_id_type=MESH,
        )

    plan = [
        (us_hbm, w_in.at[0]), (nodes_hbm, ns), (ur_hbm, w_in.at[1]), (coarse_hbm, cs),
        (uo_hbm, w_mid.at[0]), (cs_hbm, w_in.at[2]), (cr_hbm, w_in.at[3]),
        (dr_hbm, w_in.at[4]), (co_hbm, w_mid.at[1]), (ds_hbm, w_in.at[5]),
        (do_hbm, wo_full.at[0, sub]), (bs_hbm, w_in.at[6]), (br_hbm, w_in.at[7]),
        (bo_hbm, wo_full.at[1, sub]),
    ]
    loads = [
        pltpu.make_async_copy(src, dst, load_sem.at[i]) for i, (src, dst) in enumerate(plan)
    ]
    for load in loads:
        load.start()
    (l_us, l_ns, l_ur, l_cst, l_uo, l_cs, l_cr, l_dr, l_co, l_ds, l_do, l_bs, l_br, l_bo) = loads

    barrier = pltpu.get_barrier_semaphore()
    peers = [at_sub(o) for o in range(1, n_sub)]
    peers += [at_lvl(o) for o in range(1, n_lvl)]
    peers += [at_patch(o) for o in range(1, n_patch)]
    peers += [at_block(-1), at_block(1)]
    for peer in peers:
        pl.semaphore_signal(barrier, inc=1, device_id=peer, device_id_type=MESH)
    pl.semaphore_wait(barrier, len(peers))

    share = width // n_lvl

    def wo_copy(j, o, source, index):
        mine = pl.ds(pl.multiple_of(lvl * share, share), share)
        return remote(
            source.at[mine], wo_full.at[j, index, mine],
            wo_send.at[j, o - 1], wo_recv.at[j, o - 1], at_sub(o),
        )

    def wo_pass(j, o, q, owner, holder):
        part = pl.ds(pl.multiple_of(holder * share, share), share)
        return remote(
            wo_full.at[j, owner, part], wo_full.at[j, owner, part],
            fw_send.at[j, o - 1, q - 1], fw_recv.at[j, o - 1, q - 1], at_lvl(q),
        )

    wo_src = (do_hbm, bo_hbm)

    def start_wo(j):
        for o in range(1, n_sub):
            wo_copy(j, o, wo_src[j], sub).start()

    def forward_wo(j):
        for o in range(1, n_sub):
            wo_copy(j, o, wo_src[j], from_sub(o)).wait_recv()
            for q in range(1, n_lvl):
                wo_pass(j, o, q, from_sub(o), lvl).start()

    def finish_wo(j):
        for o in range(1, n_sub):
            wo_copy(j, o, wo_src[j], sub).wait_send()
            for q in range(1, n_lvl):
                wo_pass(j, o, q, from_sub(o), lvl).wait_send()
                wo_pass(j, o, q, from_sub(o), from_lvl(q)).wait_recv()

    def split_wo(j):
        for s in range(n_sub):
            high, low = split(wo_full[j, s])
            wo_pair[j, s, 0] = high
            wo_pair[j, s, 1] = low

    start_wo(0)

    def part_copy(j, o, index):
        return remote(
            parts.at[j, index], parts.at[j, index],
            part_send.at[j, o - 1], part_recv.at[j, o - 1], at_sub(o),
        )

    def send_part(j, value):
        parts[j, sub] = value
        for o in range(1, n_sub):
            part_copy(j, o, sub).start()

    def total_part(j):
        for o in range(1, n_sub):
            part_copy(j, o, sub).wait_send()
            part_copy(j, o, from_sub(o)).wait_recv()
        total = parts[j, 0]
        for s in range(1, n_sub):
            total = total + parts[j, s]
        return total

    l_us.wait()
    l_ns.wait()
    high, low = split(ns[...])
    ns_pair[0] = high
    ns_pair[1] = low
    sender = joined(split(dot3((high, low), split(w_in[0]))))
    l_ur.wait()
    l_cst.wait()
    receiver = dot3(split(cs[...]), split(w_in[1])) + ub[...]
    hid = jnp.zeros_like(receiver)
    for k in range(children.shape[1]):
        hid = hid + silu(pick(children[:, k : k + 1], sender, 0) + receiver)
    l_uo.wait()
    send_part(0, dot3(split(hid), split(w_mid[0])))

    l_dr.wait()
    rd[...] = dot3((ns_pair[0], ns_pair[1]), split(w_in[4])) + db[...]
    l_cs.wait()
    l_cr.wait()
    w_send = split(w_in[2])
    coarse_up = cs[...] + ug[...] * layer_norm(total_part(0))

    up_pair = split(coarse_up)
    table[block] = dot3(up_pair, w_send)

    def tab_copy(o, index):
        return remote(
            table.at[index], table.at[index], tab_send.at[o - 1], tab_recv.at[o - 1], at_patch(o)
        )

    def rel_copy(o, q, index):
        return remote(
            table.at[index], table.at[index],
            rel_send.at[o, q - 1], rel_recv.at[o, q - 1], at_lvl(q),
        )

    order = sorted(range(1, n_patch), key=lambda o: min(o, n_patch - o))
    for o in order:
        tab_copy(o, block).start()
    for q in range(1, n_lvl):
        rel_copy(0, q, block).start()
    receiver = dot3(up_pair, split(w_in[3])) + cb[...]
    l_bs.wait()
    l_br.wait()
    for i in range(2):
        high, low = split(w_in[6 + i])
        bw_pair[i, 0] = high
        bw_pair[i, 1] = low
    for o in order:
        tab_copy(o, from_patch(o) * n_lvl + lvl).wait_recv()
        for q in range(1, n_lvl):
            rel_copy(o, q, from_patch(o) * n_lvl + lvl).start()
    for q in range(1, n_lvl):
        rel_copy(0, q, patch * n_lvl + from_lvl(q)).wait_recv()
    for o in order:
        for q in range(1, n_lvl):
            rel_copy(o, q, from_patch(o) * n_lvl + from_lvl(q)).wait_recv()

    cells = table.shape[1]
    chunk = max(d for d in range(1, blocks + 1) if blocks % d == 0 and d * cells <= 512)
    picked = [None] * coarse_links.shape[1]
    for c in range(0, blocks, chunk):
        rows_pair = joined(split(table[c : c + chunk].reshape(chunk * cells, width)))
        for k in range(coarse_links.shape[1]):
            got = pick(coarse_links[:, k : k + 1], rows_pair, c * cells)
            picked[k] = got if picked[k] is None else picked[k] + got
    hid = jnp.zeros_like(receiver)
    for got in picked:
        hid = hid + silu(got + receiver)
    l_co.wait()
    send_part(1, dot3(split(hid), split(w_mid[1])))
    start_wo(1)
    for o in order:
        tab_copy(o, block).wait_send()
        for q in range(1, n_lvl):
            rel_copy(o, q, from_patch(o) * n_lvl + lvl).wait_send()
    for q in range(1, n_lvl):
        rel_copy(0, q, block).wait_send()

    l_do.wait()
    forward_wo(0)
    l_ds.wait()
    w_send = split(w_in[5])
    new_coarse = coarse_up + cg[...] * layer_norm(total_part(1))
    out_coarse[...] = new_coarse

    def hid_copy(j, t, o, index):
        part = pl.ds(t * tile, tile)
        return remote(
            hidden.at[j, index, part], hidden.at[j, index, part],
            hid_send.at[j, t, o - 1], hid_recv.at[j, t, o - 1], at_sub(o),
        )

    def send_hidden(j, t, value):
        hidden[j, sub, t * tile : (t + 1) * tile] = value
        for o in range(1, n_sub):
            hid_copy(j, t, o, sub).start()

    def update(j, t):
        for o in range(1, n_sub):
            hid_copy(j, t, o, from_sub(o)).wait_recv()
        total = None
        for s in range(n_sub):
            term = dot3(
                split(hidden[j, s, t * tile : (t + 1) * tile]), (wo_pair[j, s, 0], wo_pair[j, s, 1])
            )
            total = term if total is None else total + term
        return layer_norm(total)

    def interact(j, t, links, rows_pair, base, receiver):
        hid = jnp.zeros_like(receiver)
        for k in range(links.shape[1]):
            column = links[t * tile : (t + 1) * tile, k : k + 1]
            hid = hid + silu(pick(column, rows_pair, base) + receiver)
        send_hidden(j, t, hid)

    rows_pair = joined(split(dot3(split(new_coarse), w_send)))
    ends = [0, tiles - 1] + list(range(1, tiles - 1))
    for t in ends:
        interact(0, t, down_sources, rows_pair, 0, rd[t * tile : (t + 1) * tile])
    finish_wo(0)
    split_wo(0)

    def halo_copy(side):
        return remote(
            halo_out.at[side], halo_in.at[1 - side],
            halo_send.at[side], halo_recv.at[side], at_block(2 * side - 1),
        )

    for t in ends:
        part = slice(t * tile, (t + 1) * tile)
        value = ns[part] + dg[...] * update(0, t)
        nd[part] = value
        pair = split(value)
        sent = dot3(pair, (bw_pair[0, 0], bw_pair[0, 1]))
        if t == 0:
            halo_out[0] = sent[:rim]
            halo_copy(0).start()
        if t == tiles - 1:
            halo_out[1] = sent[tile - rim :]
            halo_copy(1).start()
        ext[rim + t * tile : rim + (t + 1) * tile] = joined(split(sent))
        rb[part] = dot3(pair, (bw_pair[1, 0], bw_pair[1, 1])) + bb[...]

    inner = list(range(1, tiles - 1)) + [0, tiles - 1]
    for t in inner:
        if t == 0:
            halo_copy(1).wait_recv()
            ext[:rim] = joined(split(halo_in[0]))
        if t == tiles - 1:
            halo_copy(0).wait_recv()
            ext[rim + rows :] = joined(split(halo_in[1]))
        if t == inner[1]:
            l_bo.wait()
            forward_wo(1)
        interact(
            1, t, bottom_links, ext[t * tile : (t + 1) * tile + 2 * rim], t * tile,
            rb[t * tile : (t + 1) * tile],
        )
    finish_wo(1)
    split_wo(1)
    for t in inner:
        part = slice(t * tile, (t + 1) * tile)
        out_nodes[part] = nd[part] + bg[...] * update(1, t)
    halo_copy(0).wait_send()
    halo_copy(1).wait_send()
    for j in range(2):
        for t in range(tiles):
            for o in range(1, n_sub):
                hid_copy(j, t, o, sub).wait_send()


def body(
    node_states, coarse_states, children, down_sources, bottom_links, coarse_links,
    upward_sender, upward_receiver, upward_bias, upward_output, upward_gain,
    coarse_sender, coarse_receiver, coarse_bias, coarse_output, coarse_gain,
    downward_sender, downward_receiver, downward_bias, downward_output, downward_gain,
    bottom_sender, bottom_receiver, bottom_bias, bottom_output, bottom_gain,
):
    n_patch, n_sub, n_lvl = (lax.axis_size(a) for a in ("patch", "sub", "lvl"))
    rows, lat = node_states.shape
    cells = coarse_states.shape[0]
    width = upward_sender.shape[1]
    rim = rows // 4
    tile = rim
    tiles = rows // tile
    blocks = n_patch * n_lvl
    others = n_sub - 1
    row = lambda v: v.reshape(1, -1)
    dma = pltpu.SemaphoreType.DMA
    vmem = pl.BlockSpec(memory_space=pltpu.VMEM)
    anywhere = pl.BlockSpec(memory_space=pl.ANY)
    return pl.pallas_call(
        functools.partial(kernel, n_patch, n_sub, n_lvl, rim, tile),
        out_shape=(
            jax.ShapeDtypeStruct((rows, lat), f32),
            jax.ShapeDtypeStruct((cells, lat), f32),
        ),
        in_specs=[anywhere] * 14 + [vmem] * 12,
        out_specs=(vmem, vmem),
        scratch_shapes=[
            pltpu.VMEM((rows, lat), f32),
            pltpu.VMEM((cells, lat), f32),
            pltpu.VMEM((8, lat, width), f32),
            pltpu.VMEM((2, width, lat), f32),
            pltpu.VMEM((2, n_sub, width, lat), f32),
            pltpu.VMEM((2, n_sub, 2, width, lat), bf16),
            pltpu.VMEM((2, 2, lat, width), bf16),
            pltpu.VMEM((2, rows, lat), bf16),
            pltpu.VMEM((rows, width), f32),
            pltpu.VMEM((rows, width), f32),
            pltpu.VMEM((rows, lat), f32),
            pltpu.VMEM((rows + 2 * rim, 2 * width), bf16),
            pltpu.VMEM((2, rim, width), f32),
            pltpu.VMEM((2, rim, width), f32),
            pltpu.VMEM((blocks, cells, width), f32),
            pltpu.VMEM((2, n_sub, cells, lat), f32),
            pltpu.VMEM((2, n_sub, rows, width), f32),
            dma((14,)),
            dma((2, others)),
            dma((2, others)),
            dma((2, others, n_lvl - 1)),
            dma((2, others, n_lvl - 1)),
            dma((2, others)),
            dma((2, others)),
            dma((n_patch - 1,)),
            dma((n_patch - 1,)),
            dma((n_patch, n_lvl - 1)),
            dma((n_patch, n_lvl - 1)),
            dma((2, tiles, others)),
            dma((2, tiles, others)),
            dma((2,)),
            dma((2,)),
        ],
        compiler_params=pltpu.CompilerParams(
            collective_id=0, has_side_effects=True, vmem_limit_bytes=60 * 1024 * 1024
        ),
        name="sweep",
    )(
        node_states, coarse_states,
        upward_sender, upward_receiver, upward_output,
        coarse_sender, coarse_receiver, coarse_output,
        downward_sender, downward_receiver, downward_output,
        bottom_sender, bottom_receiver, bottom_output,
        children, down_sources, bottom_links, coarse_links,
        row(upward_bias), row(upward_gain), row(coarse_bias), row(coarse_gain),
        row(downward_bias), row(downward_gain), row(bottom_bias), row(bottom_gain),
    )


def solution(mesh):
    rows = P(("parts", "patch", "lvl"), None)
    links = P(("patch", "lvl"), None)
    weights = (P(None, "sub"), P(None, "sub"), P("sub"), P("sub", None), P())
    in_specs = (rows, rows, links, links, links, links) + weights * 4
    return jax.shard_map(
        body, mesh=mesh, in_specs=in_specs, out_specs=(rows, rows), check_vma=False
    )
```

```python
import functools

import jax
import jax.numpy as jnp
from jax import lax
from jax.experimental import pallas as pl
from jax.experimental.pallas import tpu as pltpu
from jax.sharding import PartitionSpec as P

epsilon = 1e-05
f32 = jnp.float32
bf16 = jnp.bfloat16
MESH = pl.DeviceIdType.MESH


def split(x):
    high = x.astype(bf16)
    return high, (x - high.astype(f32)).astype(bf16)


def mm(a, b):
    return jnp.dot(a, b, preferred_element_type=f32)


def dot3(x, w):
    return mm(x[0], w[0]) + (mm(x[0], w[1]) + mm(x[1], w[0]))


def layer_norm(values):
    center = values - jnp.mean(values, axis=-1, keepdims=True)
    spread = jnp.mean(center * center, axis=-1, keepdims=True)
    return center * lax.rsqrt(spread + epsilon)


def silu(v):
    h = 0.5 * v
    return h + h * jnp.tanh(h)


def joined(pair):
    return jnp.concatenate(pair, axis=1)


def pick(column, table, base):
    count, width = table.shape[0], table.shape[1] // 2
    lanes = lax.broadcasted_iota(jnp.int32, (column.shape[0], count), 1)
    hot = jnp.where(lanes == column - base, 1.0, 0.0).astype(bf16)
    rows = mm(hot, table)
    return rows[:, :width] + rows[:, width:]


def kernel(
    n_patch,
    n_sub,
    n_lvl,
    rim,
    tile,
    nodes_hbm,
    coarse_hbm,
    us_hbm, ur_hbm, uo_hbm,
    cs_hbm, cr_hbm, co_hbm,
    ds_hbm, dr_hbm, do_hbm,
    bs_hbm, br_hbm, bo_hbm,
    children, down_sources, bottom_links, coarse_links,
    ub, ug, cb, cg, db, dg, bb, bg,
    out_nodes,
    out_coarse,
    ns, cs, w_in, w_mid, wo_full, wo_pair, bw_pair,
    ns_pair, rd, rb, nd, ext, halo_out, halo_in,
    table, parts, hidden,
    load_sem, wo_send, wo_recv, fw_send, fw_recv,
    part_send, part_recv, tab_send, tab_recv, rel_send, rel_recv,
    hid_send, hid_recv, halo_send, halo_recv,
):
    children, down_sources, bottom_links, coarse_links = (
        jnp.transpose(links[...]) for links in (children, down_sources, bottom_links, coarse_links)
    )
    patch = lax.axis_index("patch")
    sub = lax.axis_index("sub")
    lvl = lax.axis_index("lvl")
    rows = ns.shape[0]
    width = table.shape[2]
    tiles = rows // tile
    block = patch * n_lvl + lvl
    blocks = n_patch * n_lvl

    def at_sub(o):
        return {"sub": lax.rem(sub + o, n_sub)}

    def at_lvl(o):
        return {"lvl": lax.rem(lvl + o, n_lvl)}

    def at_patch(o):
        return {"patch": lax.rem(patch + o, n_patch)}

    def at_block(o):
        other = lax.rem(block + o + blocks, blocks)
        return {"patch": other // n_lvl, "lvl": lax.rem(other, n_lvl)}

    def from_sub(o):
        return lax.rem(sub - o + n_sub, n_sub)

    def from_patch(o):
        return lax.rem(patch - o + n_patch, n_patch)

    def from_lvl(o):
        return lax.rem(lvl - o + n_lvl, n_lvl)

    def remote(src, dst, send, recv, device):
        return pltpu.make_async_remote_copy(
            src_ref=src, dst_ref=dst, send_sem=send, recv_sem=recv,
            device_id=device, device_id_type=MESH,
        )

    plan = [
        (us_hbm, w_in.at[0]), (nodes_hbm, ns), (ur_hbm, w_in.at[1]), (coarse_hbm, cs),
        (uo_hbm, w_mid.at[0]), (cs_hbm, w_in.at[2]), (cr_hbm, w_in.at[3]),
        (dr_hbm, w_in.at[4]), (co_hbm, w_mid.at[1]), (ds_hbm, w_in.at[5]),
        (do_hbm, wo_full.at[0, sub]), (bs_hbm, w_in.at[6]), (br_hbm, w_in.at[7]),
        (bo_hbm, wo_full.at[1, sub]),
    ]
    loads = [
        pltpu.make_async_copy(src, dst, load_sem.at[i]) for i, (src, dst) in enumerate(plan)
    ]
    early = 5
    for load in loads[:early]:
        load.start()
    (l_us, l_ns, l_ur, l_cst, l_uo, l_cs, l_cr, l_dr, l_co, l_ds, l_do, l_bs, l_br, l_bo) = loads

    barrier = pltpu.get_barrier_semaphore()
    peers = [at_sub(o) for o in range(1, n_sub)]
    peers += [at_lvl(o) for o in range(1, n_lvl)]
    peers += [at_patch(o) for o in range(1, n_patch)]
    peers += [at_block(-1), at_block(1)]
    for peer in peers:
        pl.semaphore_signal(barrier, inc=1, device_id=peer, device_id_type=MESH)
    pl.semaphore_wait(barrier, len(peers))

    share = width // n_lvl

    def wo_copy(j, o, source, index):
        mine = pl.ds(pl.multiple_of(lvl * share, share), share)
        return remote(
            source.at[mine], wo_full.at[j, index, mine],
            wo_send.at[j, o - 1], wo_recv.at[j, o - 1], at_sub(o),
        )

    def wo_pass(j, o, q, owner, holder):
        part = pl.ds(pl.multiple_of(holder * share, share), share)
        return remote(
            wo_full.at[j, owner, part], wo_full.at[j, owner, part],
            fw_send.at[j, o - 1, q - 1], fw_recv.at[j, o - 1, q - 1], at_lvl(q),
        )

    wo_src = (do_hbm, bo_hbm)

    def start_wo(j):
        for o in range(1, n_sub):
            wo_copy(j, o, wo_src[j], sub).start()

    def forward_wo(j):
        for o in range(1, n_sub):
            wo_copy(j, o, wo_src[j], from_sub(o)).wait_recv()
            for q in range(1, n_lvl):
                wo_pass(j, o, q, from_sub(o), lvl).start()

    def finish_wo(j):
        for o in range(1, n_sub):
            wo_copy(j, o, wo_src[j], sub).wait_send()
            for q in range(1, n_lvl):
                wo_pass(j, o, q, from_sub(o), lvl).wait_send()
                wo_pass(j, o, q, from_sub(o), from_lvl(q)).wait_recv()

    def split_wo(j):
        for s in range(n_sub):
            high, low = split(wo_full[j, s])
            wo_pair[j, s, 0] = high
            wo_pair[j, s, 1] = low

    def part_copy(j, o, index):
        return remote(
            parts.at[j, index], parts.at[j, index],
            part_send.at[j, o - 1], part_recv.at[j, o - 1], at_sub(o),
        )

    def send_part(j, value):
        parts[j, sub] = value
        for o in range(1, n_sub):
            part_copy(j, o, sub).start()

    def total_part(j):
        for o in range(1, n_sub):
            part_copy(j, o, sub).wait_send()
            part_copy(j, o, from_sub(o)).wait_recv()
        total = parts[j, 0]
        for s in range(1, n_sub):
            total = total + parts[j, s]
        return total

    l_us.wait()
    l_ns.wait()
    for load in loads[early:]:
        load.start()
    high, low = split(ns[...])
    ns_pair[0] = high
    ns_pair[1] = low
    sender = joined(split(dot3((high, low), split(w_in[0]))))
    l_ur.wait()
    l_cst.wait()
    receiver = dot3(split(cs[...]), split(w_in[1])) + ub[...]
    hid = jnp.zeros_like(receiver)
    for k in range(children.shape[1]):
        hid = hid + silu(pick(children[:, k : k + 1], sender, 0) + receiver)
    l_uo.wait()
    send_part(0, dot3(split(hid), split(w_mid[0])))

    l_dr.wait()
    rd[...] = dot3((ns_pair[0], ns_pair[1]), split(w_in[4])) + db[...]
    l_cs.wait()
    l_cr.wait()
    w_send = split(w_in[2])
    coarse_up = cs[...] + ug[...] * layer_norm(total_part(0))

    up_pair = split(coarse_up)
    table[block] = dot3(up_pair, w_send)

    def tab_copy(o, index):
        return remote(
            table.at[index], table.at[index], tab_send.at[o - 1], tab_recv.at[o - 1], at_patch(o)
        )

    def rel_copy(o, q, index):
        return remote(
            table.at[index], table.at[index],
            rel_send.at[o, q - 1], rel_recv.at[o, q - 1], at_lvl(q),
        )

    order = sorted(range(1, n_patch), key=lambda o: min(o, n_patch - o))
    for o in order:
        tab_copy(o, block).start()
    for q in range(1, n_lvl):
        rel_copy(0, q, block).start()
    start_wo(0)
    start_wo(1)
    receiver = dot3(up_pair, split(w_in[3])) + cb[...]
    l_bs.wait()
    l_br.wait()
    for i in range(2):
        high, low = split(w_in[6 + i])
        bw_pair[i, 0] = high
        bw_pair[i, 1] = low
    for o in order:
        tab_copy(o, from_patch(o) * n_lvl + lvl).wait_recv()
        for q in range(1, n_lvl):
            rel_copy(o, q, from_patch(o) * n_lvl + lvl).start()
    for q in range(1, n_lvl):
        rel_copy(0, q, patch * n_lvl + from_lvl(q)).wait_recv()
    for o in order:
        for q in range(1, n_lvl):
            rel_copy(o, q, from_patch(o) * n_lvl + from_lvl(q)).wait_recv()

    cells = table.shape[1]
    chunk = max(d for d in range(1, blocks + 1) if blocks % d == 0 and d * cells <= 512)
    picked = [None] * coarse_links.shape[1]
    for c in range(0, blocks, chunk):
        rows_pair = joined(split(table[c : c + chunk].reshape(chunk * cells, width)))
        for k in range(coarse_links.shape[1]):
            got = pick(coarse_links[:, k : k + 1], rows_pair, c * cells)
            picked[k] = got if picked[k] is None else picked[k] + got
    hid = jnp.zeros_like(receiver)
    for got in picked:
        hid = hid + silu(got + receiver)
    l_co.wait()
    send_part(1, dot3(split(hid), split(w_mid[1])))
    for o in order:
        tab_copy(o, block).wait_send()
        for q in range(1, n_lvl):
            rel_copy(o, q, from_patch(o) * n_lvl + lvl).wait_send()
    for q in range(1, n_lvl):
        rel_copy(0, q, block).wait_send()

    l_do.wait()
    l_bo.wait()
    forward_wo(0)
    forward_wo(1)
    l_ds.wait()
    w_send = split(w_in[5])
    new_coarse = coarse_up + cg[...] * layer_norm(total_part(1))
    out_coarse[...] = new_coarse

    def hid_copy(j, t, o, index):
        part = pl.ds(t * tile, tile)
        return remote(
            hidden.at[j, index, part], hidden.at[j, index, part],
            hid_send.at[j, t, o - 1], hid_recv.at[j, t, o - 1], at_sub(o),
        )

    def send_hidden(j, t, value):
        hidden[j, sub, t * tile : (t + 1) * tile] = value
        for o in range(1, n_sub):
            hid_copy(j, t, o, sub).start()

    def update(j, t):
        for o in range(1, n_sub):
            hid_copy(j, t, o, from_sub(o)).wait_recv()
        total = None
        for s in range(n_sub):
            term = dot3(
                split(hidden[j, s, t * tile : (t + 1) * tile]), (wo_pair[j, s, 0], wo_pair[j, s, 1])
            )
            total = term if total is None else total + term
        return layer_norm(total)

    def interact(j, t, links, rows_pair, base, receiver):
        hid = jnp.zeros_like(receiver)
        for k in range(links.shape[1]):
            column = links[t * tile : (t + 1) * tile, k : k + 1]
            hid = hid + silu(pick(column, rows_pair, base) + receiver)
        send_hidden(j, t, hid)

    def halo_copy(side):
        return remote(
            halo_out.at[side], halo_in.at[1 - side],
            halo_send.at[side], halo_recv.at[side], at_block(2 * side - 1),
        )

    def descend(t):
        part = slice(t * tile, (t + 1) * tile)
        value = ns[part] + dg[...] * update(0, t)
        nd[part] = value
        pair = split(value)
        sent = dot3(pair, (bw_pair[0, 0], bw_pair[0, 1]))
        if t == 0:
            halo_out[0] = sent[:rim]
            halo_copy(0).start()
        if t == tiles - 1:
            halo_out[1] = sent[tile - rim :]
            halo_copy(1).start()
        ext[rim + t * tile : rim + (t + 1) * tile] = joined(split(sent))
        rb[part] = dot3(pair, (bw_pair[1, 0], bw_pair[1, 1])) + bb[...]

    def bottom(t):
        if t == 0:
            halo_copy(1).wait_recv()
            ext[:rim] = joined(split(halo_in[0]))
        if t == tiles - 1:
            halo_copy(0).wait_recv()
            ext[rim + rows :] = joined(split(halo_in[1]))
        interact(
            1, t, bottom_links, ext[t * tile : (t + 1) * tile + 2 * rim], t * tile,
            rb[t * tile : (t + 1) * tile],
        )

    rows_pair = joined(split(dot3(split(new_coarse), w_send)))
    for t in range(tiles):
        interact(0, t, down_sources, rows_pair, 0, rd[t * tile : (t + 1) * tile])
    for j in range(2):
        finish_wo(j)
        split_wo(j)
    for t in range(tiles):
        descend(t)
        if 2 <= t < tiles - 1:
            bottom(t - 1)
    last = list(range(max(tiles - 2, 1), tiles)) + [0]
    for t in last:
        bottom(t)
    for t in list(range(1, tiles)) + [0]:
        part = slice(t * tile, (t + 1) * tile)
        out_nodes[part] = nd[part] + bg[...] * update(1, t)
    halo_copy(0).wait_send()
    halo_copy(1).wait_send()
    for j in range(2):
        for t in range(tiles):
            for o in range(1, n_sub):
                hid_copy(j, t, o, sub).wait_send()


def body(
    node_states, coarse_states, children, down_sources, bottom_links, coarse_links,
    upward_sender, upward_receiver, upward_bias, upward_output, upward_gain,
    coarse_sender, coarse_receiver, coarse_bias, coarse_output, coarse_gain,
    downward_sender, downward_receiver, downward_bias, downward_output, downward_gain,
    bottom_sender, bottom_receiver, bottom_bias, bottom_output, bottom_gain,
):
    n_patch, n_sub, n_lvl = (lax.axis_size(a) for a in ("patch", "sub", "lvl"))
    rows, lat = node_states.shape
    cells = coarse_states.shape[0]
    width = upward_sender.shape[1]
    rim = rows // 4
    tile = rim
    tiles = rows // tile
    blocks = n_patch * n_lvl
    others = n_sub - 1
    row = lambda v: v.reshape(1, -1)
    dma = pltpu.SemaphoreType.DMA
    vmem = pl.BlockSpec(memory_space=pltpu.VMEM)
    anywhere = pl.BlockSpec(memory_space=pl.ANY)
    return pl.pallas_call(
        functools.partial(kernel, n_patch, n_sub, n_lvl, rim, tile),
        out_shape=(
            jax.ShapeDtypeStruct((rows, lat), f32),
            jax.ShapeDtypeStruct((cells, lat), f32),
        ),
        in_specs=[anywhere] * 14 + [vmem] * 12,
        out_specs=(vmem, vmem),
        scratch_shapes=[
            pltpu.VMEM((rows, lat), f32),
            pltpu.VMEM((cells, lat), f32),
            pltpu.VMEM((8, lat, width), f32),
            pltpu.VMEM((2, width, lat), f32),
            pltpu.VMEM((2, n_sub, width, lat), f32),
            pltpu.VMEM((2, n_sub, 2, width, lat), bf16),
            pltpu.VMEM((2, 2, lat, width), bf16),
            pltpu.VMEM((2, rows, lat), bf16),
            pltpu.VMEM((rows, width), f32),
            pltpu.VMEM((rows, width), f32),
            pltpu.VMEM((rows, lat), f32),
            pltpu.VMEM((rows + 2 * rim, 2 * width), bf16),
            pltpu.VMEM((2, rim, width), f32),
            pltpu.VMEM((2, rim, width), f32),
            pltpu.VMEM((blocks, cells, width), f32),
            pltpu.VMEM((2, n_sub, cells, lat), f32),
            pltpu.VMEM((2, n_sub, rows, width), f32),
            dma((14,)),
            dma((2, others)),
            dma((2, others)),
            dma((2, others, n_lvl - 1)),
            dma((2, others, n_lvl - 1)),
            dma((2, others)),
            dma((2, others)),
            dma((n_patch - 1,)),
            dma((n_patch - 1,)),
            dma((n_patch, n_lvl - 1)),
            dma((n_patch, n_lvl - 1)),
            dma((2, tiles, others)),
            dma((2, tiles, others)),
            dma((2,)),
            dma((2,)),
        ],
        compiler_params=pltpu.CompilerParams(
            collective_id=0, has_side_effects=True, vmem_limit_bytes=60 * 1024 * 1024
        ),
        name="sweep",
    )(
        node_states, coarse_states,
        upward_sender, upward_receiver, upward_output,
        coarse_sender, coarse_receiver, coarse_output,
        downward_sender, downward_receiver, downward_output,
        bottom_sender, bottom_receiver, bottom_output,
        children.T, down_sources.T, bottom_links.T, coarse_links.T,
        row(upward_bias), row(upward_gain), row(coarse_bias), row(coarse_gain),
        row(downward_bias), row(downward_gain), row(bottom_bias), row(bottom_gain),
    )


def solution(mesh):
    rows = P(("parts", "patch", "lvl"), None)
    links = P(("patch", "lvl"), None)
    weights = (P(None, "sub"), P(None, "sub"), P("sub"), P("sub", None), P())
    in_specs = (rows, rows, links, links, links, links) + weights * 4
    return jax.shard_map(
        body, mesh=mesh, in_specs=in_specs, out_specs=(rows, rows), check_vma=False
    )
```
